32 devices in a mesh: grp: 4 (over y, x), fsdp: 8 (over z, core).
Axes of the slice: x: 2, y: 2, z: 4, core: 2. Of those that a mesh axis runs over, the one named last changes fastest.
Arguments:
- tokens: bfloat16 [8192, 8192], P(('grp', 'fsdp')), may hold values from -6 to 6
- cotangent: bfloat16 [8192, 16384], P(('grp', 'fsdp')), may hold values from -6 to 6
- adapter_a: float32 [16, 16, 8192], P(None, None, 'fsdp'), may hold values from -0.0625 to 0.0625
- adapter_b: float32 [16, 16, 16384], P(None, None, 'fsdp'), may hold values from -1.5 to 1.5
- block_map: int32 [64], replicated, may hold values from 0 to 15, as said below
- adapter_owner: int32 [16], replicated, may hold values from 0 to 3, as said below
Outputs:
- delta: bfloat16 [8192, 16384], P(('grp', 'fsdp'))
- grad_tokens: bfloat16 [8192, 8192], P(('grp', 'fsdp'))
- grad_down: float32 [32, 16, 8192], P('grp', None, 'fsdp')
- grad_up: float32 [32, 16, 16384], P('grp', None, 'fsdp')
The draws below stay inside these ranges and needn't reach their ends.
Inputs may be any that keep to these rules, and one draw needn't show every extreme that they name: `block_map`: the 16 blocks of each group (blocks g * 16 to (g + 1) * 16 - 1) name exactly 4 distinct adapters. `adapter_owner`: no group owns more than 8 adapters, and one group owns exactly 8.
All inputs are finite; a program needn't handle non-finite values.
Results may differ from the reference program's by a relative error of at most 0.0065.
Values may be sent and summed in bfloat16 or wider, within the bound.
A program may use at most 128 MiB of HBM per device.

```python
import jax
import jax.numpy as jnp
from jax import lax

D = 8192
HID = 16384
RANK = 16
BLOCK = 128
ADAPTERS = 16
USED = 4
OWN_MAX = 8
BLK_GRP = 16
BLOCKS = 64
TOKENS = 8192
N_GRP = 4


def draw_block_map(key, part):

    def one_group(group_id):
        group_key = jax.random.fold_in(key, group_id)
        subkeys = jax.random.split(group_key, 3)
        chosen = jax.random.permutation(subkeys[0], ADAPTERS)[:USED]
        assigned = jax.random.randint(subkeys[1], (BLK_GRP,), 0, USED)
        assigned = assigned.at[:USED].set(jnp.arange(USED))
        assigned = assigned[jax.random.permutation(subkeys[2], BLK_GRP)]
        return chosen[assigned].astype(jnp.int32)
    return jax.vmap(one_group)(jnp.arange(N_GRP)).reshape(BLOCKS).astype(jnp.int32)


def draw_adapter_owner(key, part):
    subkeys = jax.random.split(jax.random.fold_in(key, 7), 3)
    shuffled = jax.random.permutation(subkeys[0], ADAPTERS)
    heavy_group = jax.random.randint(subkeys[1], (), 0, N_GRP)
    others = jax.random.randint(subkeys[2], (ADAPTERS,), 0, N_GRP - 1)
    others = others + (others >= heavy_group).astype(jnp.int32)
    ranked = jnp.where(jnp.arange(ADAPTERS) < OWN_MAX, heavy_group, others).astype(jnp.int32)
    return jnp.zeros((ADAPTERS,), jnp.int32).at[shuffled].set(ranked)


def block_levels(key, shape, cuts, low, largest):
    def one(axis_at, blocks):
        heights = jax.random.uniform(jax.random.fold_in(jax.random.fold_in(key, 6), axis_at), (blocks,), jnp.float32, low / len(cuts), largest / len(cuts))
        return jnp.repeat(jnp.exp(heights), shape[axis_at] // blocks).reshape((-1,) + (1,) * (len(shape) - axis_at - 1))

    level = one(*cuts[0])
    for cut in cuts[1:]:
        level = level * one(*cut)
    return level


def gaussian(key, shape, scale, reach, cuts=(), held_as=jnp.bfloat16):
    level = block_levels(key, shape, cuts, -0.22, 0.18) if cuts else 1.0
    entries = jax.random.normal(key, shape, jnp.float32) * scale * level
    return jnp.minimum(jnp.maximum(entries, -reach), reach).astype(held_as)


def setup_inputs(seed: int = 0) -> dict:
    splits = jax.random.split(jax.random.key(seed), 7)
    return {
        "tokens": gaussian(splits[0], (TOKENS, D), 1.0, 6.0, ((0, 32),)),
        "cotangent": gaussian(splits[1], (TOKENS, HID), 1.0, 6.0, ((0, 32),)),
        "adapter_a": gaussian(splits[2], (ADAPTERS, RANK, D), D ** -0.5, 0.0625, ((2, 8),), jnp.float32),
        "adapter_b": gaussian(splits[3], (ADAPTERS, RANK, HID), RANK ** -0.5, 1.5, ((2, 8),), jnp.float32),
        "block_map": draw_block_map(jax.random.fold_in(splits[6], 71), 0),
        "adapter_owner": draw_adapter_owner(jax.random.fold_in(splits[6], 71), 0),
    }


def ordered_members(members, slot_count):
    total = members.shape[-1]
    position = (jnp.cumsum(members, axis=-1) - 1).astype(jnp.int32)
    slot_range = jnp.arange(slot_count, dtype=jnp.int32)
    matches = (members[..., None, :] == 1) & (position[..., None, :] == slot_range[:, None])
    catalog = jnp.arange(total, dtype=jnp.int32)
    found = jnp.sum(jnp.where(matches, catalog, 0), axis=-1).astype(jnp.int32)
    return jnp.where(jnp.any(matches, axis=-1), found, -1).astype(jnp.int32)


def reference(tokens, cotangent, adapter_a, adapter_b, block_map, adapter_owner):
    down_low = adapter_a.astype(jnp.bfloat16)
    up_low = adapter_b.astype(jnp.bfloat16)
    blocks = block_map.shape[0]
    tok_blocks = tokens.reshape(blocks, BLOCK, D)
    cot_blocks = cotangent.reshape(blocks, BLOCK, HID)

    def advance(totals, pieces):
        sum_a, sum_b = totals
        tok_piece, cot_piece, adapter_id = pieces
        down_one = down_low[adapter_id]
        up_one = up_low[adapter_id]
        low_rank = jnp.dot(tok_piece, down_one.T, preferred_element_type=jnp.float32).astype(jnp.bfloat16)
        delta_piece = jnp.dot(low_rank, up_one, preferred_element_type=jnp.float32).astype(jnp.bfloat16)
        back_rank = jnp.dot(cot_piece, up_one.T, preferred_element_type=jnp.float32).astype(jnp.bfloat16)
        grad_piece = jnp.dot(back_rank, down_one, preferred_element_type=jnp.float32).astype(jnp.bfloat16)
        down_part = jnp.dot(back_rank.T, tok_piece, preferred_element_type=jnp.float32)
        up_part = jnp.dot(low_rank.T, cot_piece, preferred_element_type=jnp.float32)
        sum_a = sum_a.at[adapter_id].add(down_part)
        sum_b = sum_b.at[adapter_id].add(up_part)
        return (sum_a, sum_b), (delta_piece, grad_piece)

    start_a = jnp.zeros((ADAPTERS, RANK, D), jnp.float32)
    start_b = jnp.zeros((ADAPTERS, RANK, HID), jnp.float32)
    (sum_a, sum_b), (delta_blocks, grad_blocks) = lax.scan(
        advance, (start_a, start_b), (tok_blocks, cot_blocks, block_map.astype(jnp.int32)))
    catalog = jnp.arange(ADAPTERS, dtype=jnp.int32)
    uses = jnp.sum((block_map[:, None] == catalog[None, :]).astype(jnp.int32), axis=0).astype(jnp.int32)
    divisor = (BLOCK * jnp.maximum(uses, 1)).astype(jnp.float32)
    sum_down = sum_a / divisor[:, None, None]
    sum_up = sum_b / divisor[:, None, None]
    owner_marks = (adapter_owner[None, :] == jnp.arange(N_GRP, dtype=jnp.int32)[:, None]).astype(jnp.int32)
    owned = ordered_members(owner_marks, OWN_MAX).reshape(N_GRP * OWN_MAX)
    filled = (owned >= 0).astype(jnp.float32)
    safe_ids = jnp.maximum(owned, 0).astype(jnp.int32)
    grad_down = sum_down[safe_ids] * filled[:, None, None]
    grad_up = sum_up[safe_ids] * filled[:, None, None]
    delta = delta_blocks.reshape(blocks * BLOCK, HID)
    grad_tokens = grad_blocks.reshape(blocks * BLOCK, D)
    return (delta, grad_tokens, grad_down, grad_up)
```

```python
import functools

import jax
import jax.numpy as jnp
from jax import lax
from jax.experimental import pallas as pl
from jax.experimental.pallas import tpu as pltpu
from jax.sharding import PartitionSpec as P

BLOCK = 128
USED = 4
OWN_MAX = 8
RANK = 16
ROWS = USED * RANK
MESH = pl.DeviceIdType.MESH
NT = (((1,), (1,)), ((), ()))
PIECES = 3
RIGHT, LEFT, PARTNER = 0, 1, 2
BF16, F32 = jnp.bfloat16, jnp.float32


def used_adapters(bm, base, count, last_name):
    found = []
    for _ in range(USED):
        def smallest(i, best, last=found[-1] if found else -1):
            entry = bm[base + i]
            return jnp.where((entry > last) & (entry < best), entry, best)

        found.append(lax.fori_loop(0, count, smallest, jnp.int32(last_name), unroll=min(count, 16)))
    return found


def exchange(
    groups, shards,
    bm, owners, a_hbm, b_hbm, tokens, cotangent,
    low_out, back_out, pick_out, scale_out, wd_out, wu_out, shares_out,
    a_f32, b_f32, wd, wu_low, wu_high, tok, cot, acc, left_t,
    to_mate, from_mate, own_part, arrived, running, final,
    load_sem, tok_sem, cot_sem, store_sem, ag_send, ag_recv,
    mate_send, mate_recv, run_send, run_recv, grp_send, grp_recv, keep_sem,
):
    line = shards // 2
    g = lax.axis_index("grp")
    f = lax.axis_index("fsdp")
    z = f // 2
    c = f % 2
    mate = z * 2 + (1 - c)
    wp = a_hbm.shape[2]
    rows = tokens.shape[0]
    blocks_dev = rows // BLOCK
    total_blocks = bm.shape[0]
    group_blocks = total_blocks // groups
    adapters = a_hbm.shape[0]
    has_left, has_right = z > 0, z < line - 1
    at_end = (z == 0) | (z == line - 1)

    maps = (wd, wu_low, wu_high)

    barrier = pltpu.get_barrier_semaphore()

    def greet(target):
        pl.semaphore_signal(barrier, inc=1, device_id=target, device_id_type=MESH)

    greet((g, mate))
    pl.when(has_left)(lambda: greet((g, f - 2)))
    pl.when(has_right)(lambda: greet((g, f + 2)))
    for step in range(1, groups):
        greet(((g + step) % groups, f))

    load_a = pltpu.make_async_copy(a_hbm, a_f32, load_sem.at[0])
    load_b = pltpu.make_async_copy(b_hbm, b_f32, load_sem.at[1])
    load_a.start()
    load_b.start()

    def load_tok(s):
        return pltpu.make_async_copy(
            tokens.at[:, pl.ds(pl.multiple_of(s * wp, 128), wp)], tok.at[s], tok_sem.at[s]
        )

    def load_cot(s):
        return pltpu.make_async_copy(
            cotangent.at[:, pl.ds(pl.multiple_of(s * 2 * wp, 128), 2 * wp)], cot.at[s], cot_sem.at[s]
        )

    for s in range(shards):
        load_tok(s).start()
    for s in range(shards):
        load_cot(s).start()

    used = used_adapters(bm, g * group_blocks, group_blocks, adapters - 1)

    def weights(piece, shard):
        return maps[piece].at[shard]

    def gather_copy(piece, origin, way):
        ref = weights(piece, origin)
        target = {RIGHT: f + 2, LEFT: f - 2, PARTNER: mate}[way]
        return pltpu.make_async_remote_copy(
            src_ref=ref, dst_ref=ref,
            send_sem=ag_send.at[way, piece, origin // 2],
            recv_sem=ag_recv.at[piece, origin],
            device_id=(g, target), device_id_type=MESH,
        )

    def gather_own(piece):
        pl.when(has_right)(lambda: gather_copy(piece, f, RIGHT).start())
        pl.when(has_left)(lambda: gather_copy(piece, f, LEFT).start())
        gather_copy(piece, f, PARTNER).start()

    def accumulate(piece):
        def body(s, _):
            if piece == 0:
                values = tok[s]
            else:
                values = cot[s, :, (piece - 1) * wp:piece * wp]
            acc[...] += lax.dot_general(values, maps[piece][s], NT, preferred_element_type=F32)
            return 0

        lax.fori_loop(0, shards, body, 0, unroll=4)

    def gather_span(piece, first, last):
        def body(q, _):
            same = 1 - (q % 4) // 2
            side = 2 * (q % 2) - 1
            dist = q // 4 + same
            place = z + side * dist
            here = (place >= 0) & (place < line) & ((side < 0) | (dist > 0))
            origin = place * 2 + (c + 1 - same) % 2

            @pl.when(here)
            def _():
                gather_copy(piece, origin, PARTNER).wait_recv()

                @pl.when((same == 1) & (side < 0) & has_right)
                def _():
                    gather_copy(piece, origin, RIGHT).start()

                @pl.when((same == 1) & (side > 0) & has_left)
                def _():
                    gather_copy(piece, origin, LEFT).start()

                @pl.when(same == 1)
                def _():
                    gather_copy(piece, origin, PARTNER).start()

            return 0

        lax.fori_loop(first, last, body, 0)

    def gather_finish(piece):
        def body(place, _):
            origin = place * 2 + c
            pl.when((place <= z) & has_right)(
                lambda: gather_copy(piece, origin, RIGHT).wait_send()
            )
            pl.when((place >= z) & has_left)(
                lambda: gather_copy(piece, origin, LEFT).wait_send()
            )
            gather_copy(piece, origin, PARTNER).wait_send()
            return 0

        lax.fori_loop(0, line, body, 0)

    def masked(total):
        row = lax.broadcasted_iota(jnp.int32, (rows, ROWS), 0) // BLOCK
        slot = lax.broadcasted_iota(jnp.int32, (rows, ROWS), 1) // RANK
        wanted = jnp.zeros((rows, ROWS), jnp.int32)
        for b in range(blocks_dev):
            entry = bm[(g * shards + f) * blocks_dev + b]
            place = jnp.int32(0)
            for s in range(1, USED):
                place = jnp.where(entry == used[s], s, place)
            wanted = jnp.where(row == b, place, wanted)
        return jnp.where(slot == wanted, total, 0.0)

    steps = [(side, dist) for dist in range(line - 1, 0, -1) for side in (1, -1)] + [(1, 0)]
    number = {step: i for i, step in enumerate(steps)}
    last = number[(1, 0)]

    def here(step):
        side, dist = step
        return z + dist < line if side > 0 else z - dist >= 0

    def mate_copy(p, i):
        return pltpu.make_async_remote_copy(
            src_ref=to_mate.at[p, i], dst_ref=from_mate.at[p, i],
            send_sem=mate_send.at[p, i], recv_sem=mate_recv.at[p, i],
            device_id=(g, mate), device_id_type=MESH,
        )

    def partials(pieces, values):
        for i, (side, dist) in enumerate(steps):
            d = z + side * dist

            @pl.when(here((side, dist)))
            def _():
                given = jnp.dot(
                    left_t[...], values[d * 2 + (1 - c)], preferred_element_type=F32
                )
                for n, p in enumerate(pieces):
                    to_mate[p, i] = given[:, n * wp:(n + 1) * wp].astype(BF16)
                for p in pieces:
                    mate_copy(p, i).start()
                kept = jnp.dot(left_t[...], values[d * 2 + c], preferred_element_type=F32)
                for n, p in enumerate(pieces):
                    own_part[p, i] = kept[:, n * wp:(n + 1) * wp]

    def run_copy(p, side, dist):
        row = (1 - side) // 2
        return pltpu.make_async_remote_copy(
            src_ref=running.at[p, number[(side, dist)]], dst_ref=arrived.at[p, row, dist - 1],
            send_sem=run_send.at[p, number[(side, dist)]], recv_sem=run_recv.at[p, row, dist - 1],
            device_id=(g, f + 2 * side), device_id_type=MESH,
        )

    def run_wait(p, side, dist):
        run_copy(p, side, dist + 1).wait_recv()
        return arrived[p, (1 - side) // 2, dist].astype(F32)

    def pass_on(pieces):
        for i, (side, dist) in enumerate(steps[:-1]):
            fed = has_left if side > 0 else has_right

            @pl.when(here((side, dist)))
            def _():
                for p in pieces:
                    mate_copy(p, i).wait_recv()
                    if dist < line - 1:
                        @pl.when(fed)
                        def _():
                            running[p, i] = (
                                own_part[p, i]
                                + from_mate[p, i].astype(F32)
                                + run_wait(p, side, dist)
                            ).astype(BF16)

                        @pl.when(jnp.logical_not(fed))
                        def _():
                            running[p, i] = (
                                own_part[p, i] + from_mate[p, i].astype(F32)
                            ).astype(BF16)
                    else:
                        running[p, i] = (own_part[p, i] + from_mate[p, i].astype(F32)).astype(
                            BF16
                        )
                    run_copy(p, side, dist).start()

    def grp_copy(p, step):
        return pltpu.make_async_remote_copy(
            src_ref=final.at[p], dst_ref=shares_out.at[p, g],
            send_sem=grp_send.at[p, step], recv_sem=grp_recv.at[p, g],
            device_id=((g + step) % groups, f), device_id_type=MESH,
        )

    def grp_wait(p, other):
        pltpu.make_async_remote_copy(
            src_ref=final.at[p], dst_ref=shares_out.at[p, other],
            send_sem=grp_send.at[p, 0], recv_sem=grp_recv.at[p, other],
            device_id=(g, mate), device_id_type=MESH,
        ).wait_recv()

    def keep_copy(p):
        return pltpu.make_async_copy(final.at[p], shares_out.at[p, g], keep_sem.at[p])

    def finish_piece(p):
        mate_copy(p, last).wait_recv()
        own_part[p, last] += from_mate[p, last].astype(F32)

        @pl.when(has_left)
        def _():
            own_part[p, last] += run_wait(p, 1, 0)

        @pl.when(has_right)
        def _():
            own_part[p, last] += run_wait(p, -1, 0)

        final[p] = own_part[p, last].astype(BF16)
        for step in range(1, groups):
            grp_copy(p, step).start()
        keep_copy(p).start()

    load_a.wait()
    wd[f] = jnp.concatenate([a_f32[u].astype(BF16) for u in used], axis=0)
    pl.semaphore_wait(
        barrier, groups + jnp.where(has_left, 1, 0) + jnp.where(has_right, 1, 0)
    )
    gather_own(0)
    load_b.wait()
    for half in range(2):
        maps[1 + half][f] = jnp.concatenate(
            [b_f32[u, :, half * wp:(half + 1) * wp].astype(BF16) for u in used], axis=0
        )
    acc[...] = jnp.zeros_like(acc)
    gather_span(0, 0, 2)
    gather_own(1)
    gather_span(0, 2, 4 * line)
    gather_own(2)
    for s in range(shards):
        load_tok(s).wait()
    accumulate(0)
    low = masked(acc[...])
    low_out[...] = low.astype(BF16)
    left_t[...] = low.T.astype(BF16)
    for s in range(shards):
        load_cot(s).wait()
    partials((0, 1), cot)
    pl.when(at_end)(lambda: pass_on((0, 1)))

    acc[...] = jnp.zeros_like(acc)
    gather_span(1, 0, 4 * line)
    accumulate(1)
    gather_span(2, 0, 4 * line)
    accumulate(2)
    back = masked(acc[...])
    back_out[...] = back.astype(BF16)
    left_t[...] = back.T.astype(BF16)
    partials((2,), tok)
    pl.when(at_end)(lambda: pass_on((2,)))
    pl.when(jnp.logical_not(at_end))(lambda: pass_on((0, 1)))

    store_d = pltpu.make_async_copy(wd, wd_out, store_sem.at[0])
    store_l = pltpu.make_async_copy(wu_low, wu_out.at[0], store_sem.at[1])
    store_h = pltpu.make_async_copy(wu_high, wu_out.at[1], store_sem.at[2])
    store_d.start()
    store_l.start()
    store_h.start()

    finish_piece(0)
    finish_piece(1)
    pl.when(jnp.logical_not(at_end))(lambda: pass_on((2,)))

    names = [
        used_adapters(bm, other * group_blocks, group_blocks, adapters - 1)
        for other in range(groups)
    ]
    owned = [jnp.int32(-1)] * OWN_MAX
    position = jnp.int32(0)
    for a in range(adapters):
        mine = owners[a] == g
        for k in range(OWN_MAX):
            owned[k] = jnp.where(mine & (position == k), a, owned[k])
        position = position + jnp.where(mine, 1, 0)

    def count(i, totals):
        entry = bm[i]
        return tuple(n + jnp.where(entry == o, 1, 0) for n, o in zip(totals, owned))

    totals = lax.fori_loop(0, total_blocks, count, (jnp.int32(0),) * OWN_MAX, unroll=8)
    shape = (OWN_MAX * RANK, groups * ROWS)
    row = lax.broadcasted_iota(jnp.int32, shape, 0)
    col = lax.broadcasted_iota(jnp.int32, shape, 1)
    row_name = jnp.full(shape, -1, jnp.int32)
    col_name = jnp.full(shape, -2, jnp.int32)
    for k in range(OWN_MAX):
        row_name = jnp.where(row // RANK == k, owned[k], row_name)
    for q in range(groups * USED):
        col_name = jnp.where(col // RANK == q, names[q // USED][q % USED], col_name)
    hit = (row % RANK == col % RANK) & (row_name == col_name)
    pick_out[...] = jnp.where(hit, 1.0, 0.0).astype(BF16)
    wide = lax.broadcasted_iota(jnp.int32, scale_out.shape, 0) // RANK
    uses = jnp.zeros(scale_out.shape, jnp.int32)
    for k in range(OWN_MAX):
        uses = jnp.where(wide == k, totals[k], uses)
    scale_out[...] = 1.0 / (BLOCK * jnp.maximum(uses, 1)).astype(F32)

    finish_piece(2)
    for piece in range(PIECES):
        gather_finish(piece)

    for i, step in enumerate(steps):
        @pl.when(here(step))
        def _():
            for p in range(PIECES):
                mate_copy(p, i).wait_send()
                if i != last:
                    run_copy(p, *step).wait_send()

    store_d.wait()
    store_l.wait()
    store_h.wait()
    for p in range(PIECES):
        keep_copy(p).wait()
        for step in range(1, groups):
            grp_copy(p, step).wait_send()
        for step in range(1, groups):
            grp_wait(p, (g + step) % groups)


def outputs(
    low, back, pick, scale, wd, wu, up_shares, down_shares,
    delta, grad_tokens, grad_down, grad_up,
):
    count, _, wp = wd.shape
    for s in range(count):
        for half in range(2):
            start = (s * 2 + half) * wp
            delta[:, start:start + wp] = jnp.dot(
                low[...], wu[half, s], preferred_element_type=F32
            ).astype(delta.dtype)
        grad_tokens[:, s * wp:(s + 1) * wp] = jnp.dot(
            back[...], wd[s], preferred_element_type=F32
        ).astype(grad_tokens.dtype)
    for shares, grad in ((down_shares, grad_down), (up_shares, grad_up)):
        total = jnp.dot(pick[...], shares[0], preferred_element_type=F32)
        grad[...] = (total * scale[:, 0:1]).reshape(grad.shape)


def on_device(groups, shards, tokens, cotangent, adapter_a, adapter_b, block_map, adapter_owner):
    rows, width = tokens.shape
    hidden = cotangent.shape[1]
    wp = adapter_a.shape[2]
    assert adapter_b.shape[2] == 2 * wp
    line = shards // 2
    dma = pltpu.SemaphoreType.DMA
    vmem = pl.BlockSpec(memory_space=pltpu.VMEM)
    smem = pl.BlockSpec(memory_space=pltpu.SMEM)
    anywhere = pl.BlockSpec(memory_space=pl.ANY)
    low, back, pick, scale, wd, wu, shares = pl.pallas_call(
        functools.partial(exchange, groups, shards),
        name="exchange",
        out_shape=(
            jax.ShapeDtypeStruct((rows, ROWS), BF16),
            jax.ShapeDtypeStruct((rows, ROWS), BF16),
            jax.ShapeDtypeStruct((OWN_MAX * RANK, groups * ROWS), BF16),
            jax.ShapeDtypeStruct((OWN_MAX * RANK, 128), F32),
            jax.ShapeDtypeStruct((shards, ROWS, wp), BF16),
            jax.ShapeDtypeStruct((2, shards, ROWS, wp), BF16),
            jax.ShapeDtypeStruct((PIECES, groups, ROWS, wp), BF16),
        ),
        in_specs=[smem, smem] + [anywhere] * 4,
        out_specs=(vmem,) * 4 + (anywhere,) * 3,
        scratch_shapes=[
            pltpu.VMEM(adapter_a.shape, F32),
            pltpu.VMEM(adapter_b.shape, F32),
            pltpu.VMEM((shards, ROWS, wp), BF16),
            pltpu.VMEM((shards, ROWS, wp), BF16),
            pltpu.VMEM((shards, ROWS, wp), BF16),
            pltpu.VMEM((shards, rows, wp), BF16),
            pltpu.VMEM((shards, rows, 2 * wp), BF16),
            pltpu.VMEM((rows, ROWS), F32),
            pltpu.VMEM((ROWS, rows), BF16),
            pltpu.VMEM((PIECES, 2 * line - 1, ROWS, wp), BF16),
            pltpu.VMEM((PIECES, 2 * line - 1, ROWS, wp), BF16),
            pltpu.VMEM((PIECES, 2 * line - 1, ROWS, wp), F32),
            pltpu.VMEM((PIECES, 2, line, ROWS, wp), BF16),
            pltpu.VMEM((PIECES, 2 * line - 1, ROWS, wp), BF16),
            pltpu.VMEM((PIECES, ROWS, wp), BF16),
            dma((2,)),
            dma((shards,)),
            dma((shards,)),
            dma((3,)),
            dma((3, PIECES, line)),
            dma((PIECES, shards)),
            dma((PIECES, 2 * line - 1)),
            dma((PIECES, 2 * line - 1)),
            dma((PIECES, 2 * line - 1)),
            dma((PIECES, 2, line)),
            dma((PIECES, groups)),
            dma((PIECES, groups)),
            dma((PIECES,)),
        ],
        compiler_params=pltpu.CompilerParams(
            collective_id=0, has_side_effects=True, vmem_limit_bytes=56 * 1024 * 1024
        ),
    )(block_map, adapter_owner, adapter_a, adapter_b, tokens, cotangent)
    shares = shares.reshape(PIECES, groups * ROWS, wp)
    steps = min(4, wp // 128)
    half = steps // 2
    whole = lambda shape: pl.BlockSpec(shape, lambda i: (0,) * len(shape))
    return pl.pallas_call(
        outputs,
        name="outputs",
        grid=(steps,),
        out_shape=(
            jax.ShapeDtypeStruct((rows, hidden), BF16),
            jax.ShapeDtypeStruct((rows, width), BF16),
            jax.ShapeDtypeStruct((OWN_MAX, RANK, wp), F32),
            jax.ShapeDtypeStruct((OWN_MAX, RANK, 2 * wp), F32),
        ),
        in_specs=[
            whole(low.shape), whole(back.shape), whole(pick.shape), whole(scale.shape),
            pl.BlockSpec((shards // steps, ROWS, wp), lambda i: (i, 0, 0)),
            pl.BlockSpec((2, shards // steps, ROWS, wp), lambda i: (0, i, 0, 0)),
            pl.BlockSpec((1, groups * ROWS, wp // half), lambda i: (i // half, 0, i % half)),
            pl.BlockSpec((1, groups * ROWS, wp // steps), lambda i: (2, 0, i)),
        ],
        out_specs=(
            pl.BlockSpec((rows, hidden // steps), lambda i: (0, i)),
            pl.BlockSpec((rows, width // steps), lambda i: (0, i)),
            pl.BlockSpec((OWN_MAX, RANK, wp // steps), lambda i: (0, 0, i)),
            pl.BlockSpec((OWN_MAX, RANK, 2 * wp // steps), lambda i: (0, 0, i)),
        ),
    )(low, back, pick, scale, wd, wu, shares, shares)


def solution(mesh):
    placed = (
        P(("grp", "fsdp"), None),
        P(("grp", "fsdp"), None),
        P(None, None, "fsdp"),
        P(None, None, "fsdp"),
        P(),
        P(),
    )
    return jax.shard_map(
        functools.partial(on_device, mesh.shape["grp"], mesh.shape["fsdp"]),
        mesh=mesh,
        in_specs=placed,
        out_specs=(
            P(("grp", "fsdp"), None),
            P(("grp", "fsdp"), None),
            P("grp", None, "fsdp"),
            P("grp", None, "fsdp"),
        ),
        check_vma=False,
    )
```

```python
import functools

import jax
import jax.numpy as jnp
from jax import lax
from jax.experimental import pallas as pl
from jax.experimental.pallas import tpu as pltpu
from jax.sharding import PartitionSpec as P

BLOCK = 128
USED = 4
OWN_MAX = 8
RANK = 16
ROWS = USED * RANK
MESH = pl.DeviceIdType.MESH
NT = (((1,), (1,)), ((), ()))
PIECES = 3
RIGHT, LEFT, PARTNER = 0, 1, 2
BF16, F32 = jnp.bfloat16, jnp.float32


def used_adapters(bm, base, count, last_name):
    found = []
    for _ in range(USED):
        def smallest(i, best, last=found[-1] if found else -1):
            entry = bm[base + i]
            return jnp.where((entry > last) & (entry < best), entry, best)

        found.append(lax.fori_loop(0, count, smallest, jnp.int32(last_name), unroll=min(count, 16)))
    return found


def exchange(
    groups, shards,
    bm, owners, a_hbm, b_hbm, tokens, cotangent,
    low_out, back_out, pick_out, scale_out, wd_out, wu_out, shares_out,
    a_f32, b_f32, wd, wu_low, wu_high, tok, cot, acc, left_t,
    to_mate, from_mate, own_part, arrived, running, final,
    load_sem, tok_sem, cot_sem, store_sem, ag_send, ag_recv,
    mate_send, mate_recv, run_send, run_recv, grp_send, grp_recv, keep_sem,
):
    line = shards // 2
    g = lax.axis_index("grp")
    f = lax.axis_index("fsdp")
    z = f // 2
    c = f % 2
    mate = z * 2 + (1 - c)
    wp = a_hbm.shape[2]
    rows = tokens.shape[0]
    blocks_dev = rows // BLOCK
    total_blocks = bm.shape[0]
    group_blocks = total_blocks // groups
    adapters = a_hbm.shape[0]
    has_left, has_right = z > 0, z < line - 1
    at_end = (z == 0) | (z == line - 1)

    maps = (wd, wu_low, wu_high)

    barrier = pltpu.get_barrier_semaphore()

    def greet(target):
        pl.semaphore_signal(barrier, inc=1, device_id=target, device_id_type=MESH)

    greet((g, mate))
    pl.when(has_left)(lambda: greet((g, f - 2)))
    pl.when(has_right)(lambda: greet((g, f + 2)))
    for step in range(1, groups):
        greet(((g + step) % groups, f))

    load_a = pltpu.make_async_copy(a_hbm, a_f32, load_sem.at[0])
    load_b = pltpu.make_async_copy(b_hbm, b_f32, load_sem.at[1])
    load_a.start()
    load_b.start()

    def load_tok(s):
        return pltpu.make_async_copy(
            tokens.at[:, pl.ds(pl.multiple_of(s * wp, 128), wp)], tok.at[s], tok_sem.at[s]
        )

    def load_cot(s):
        return pltpu.make_async_copy(
            cotangent.at[:, pl.ds(pl.multiple_of(s * 2 * wp, 128), 2 * wp)], cot.at[s], cot_sem.at[s]
        )

    used = used_adapters(bm, g * group_blocks, group_blocks, adapters - 1)

    def weights(piece, shard):
        return maps[piece].at[shard]

    def gather_copy(piece, origin, way):
        ref = weights(piece, origin)
        target = {RIGHT: f + 2, LEFT: f - 2, PARTNER: mate}[way]
        return pltpu.make_async_remote_copy(
            src_ref=ref, dst_ref=ref,
            send_sem=ag_send.at[way, piece, origin // 2],
            recv_sem=ag_recv.at[piece, origin],
            device_id=(g, target), device_id_type=MESH,
        )

    def gather_own(piece):
        pl.when(has_right)(lambda: gather_copy(piece, f, RIGHT).start())
        pl.when(has_left)(lambda: gather_copy(piece, f, LEFT).start())
        gather_copy(piece, f, PARTNER).start()

    def accumulate(piece):
        def body(s, _):
            if piece == 0:
                values = tok[s]
            else:
                values = cot[s, :, (piece - 1) * wp:piece * wp]
            acc[...] += lax.dot_general(values, maps[piece][s], NT, preferred_element_type=F32)
            return 0

        lax.fori_loop(0, shards, body, 0, unroll=4)

    def gather_span(piece, first, last):
        def body(q, _):
            same = 1 - (q % 4) // 2
            side = 2 * (q % 2) - 1
            dist = q // 4 + same
            place = z + side * dist
            here = (place >= 0) & (place < line) & ((side < 0) | (dist > 0))
            origin = place * 2 + (c + 1 - same) % 2

            @pl.when(here)
            def _():
                gather_copy(piece, origin, PARTNER).wait_recv()

                @pl.when((same == 1) & (side < 0) & has_right)
                def _():
                    gather_copy(piece, origin, RIGHT).start()

                @pl.when((same == 1) & (side > 0) & has_left)
                def _():
                    gather_copy(piece, origin, LEFT).start()

                @pl.when(same == 1)
                def _():
                    gather_copy(piece, origin, PARTNER).start()

            return 0

        lax.fori_loop(first, last, body, 0)

    def gather_finish(piece):
        def body(place, _):
            origin = place * 2 + c
            pl.when((place <= z) & has_right)(
                lambda: gather_copy(piece, origin, RIGHT).wait_send()
            )
            pl.when((place >= z) & has_left)(
                lambda: gather_copy(piece, origin, LEFT).wait_send()
            )
            gather_copy(piece, origin, PARTNER).wait_send()
            return 0

        lax.fori_loop(0, line, body, 0)

    def masked(total):
        row = lax.broadcasted_iota(jnp.int32, (rows, ROWS), 0) // BLOCK
        slot = lax.broadcasted_iota(jnp.int32, (rows, ROWS), 1) // RANK
        wanted = jnp.zeros((rows, ROWS), jnp.int32)
        for b in range(blocks_dev):
            entry = bm[(g * shards + f) * blocks_dev + b]
            place = jnp.int32(0)
            for s in range(1, USED):
                place = jnp.where(entry == used[s], s, place)
            wanted = jnp.where(row == b, place, wanted)
        return jnp.where(slot == wanted, total, 0.0)

    steps = [(side, dist) for dist in range(line - 1, 0, -1) for side in (1, -1)] + [(1, 0)]
    number = {step: i for i, step in enumerate(steps)}
    last = number[(1, 0)]

    def here(step):
        side, dist = step
        return z + dist < line if side > 0 else z - dist >= 0

    def mate_copy(p, i):
        return pltpu.make_async_remote_copy(
            src_ref=to_mate.at[p, i], dst_ref=from_mate.at[p, i],
            send_sem=mate_send.at[p, i], recv_sem=mate_recv.at[p, i],
            device_id=(g, mate), device_id_type=MESH,
        )

    def partials(pieces, values):
        for i, (side, dist) in enumerate(steps):
            d = z + side * dist

            @pl.when(here((side, dist)))
            def _():
                given = jnp.dot(
                    left_t[...], values[d * 2 + (1 - c)], preferred_element_type=F32
                )
                for n, p in enumerate(pieces):
                    to_mate[p, i] = given[:, n * wp:(n + 1) * wp].astype(BF16)
                for p in pieces:
                    mate_copy(p, i).start()
                kept = jnp.dot(left_t[...], values[d * 2 + c], preferred_element_type=F32)
                for n, p in enumerate(pieces):
                    own_part[p, i] = kept[:, n * wp:(n + 1) * wp]

    def run_copy(p, side, dist):
        row = (1 - side) // 2
        return pltpu.make_async_remote_copy(
            src_ref=running.at[p, number[(side, dist)]], dst_ref=arrived.at[p, row, dist - 1],
            send_sem=run_send.at[p, number[(side, dist)]], recv_sem=run_recv.at[p, row, dist - 1],
            device_id=(g, f + 2 * side), device_id_type=MESH,
        )

    def run_wait(p, side, dist):
        run_copy(p, side, dist + 1).wait_recv()
        return arrived[p, (1 - side) // 2, dist].astype(F32)

    def pass_on(pieces):
        for i, (side, dist) in enumerate(steps[:-1]):
            fed = has_left if side > 0 else has_right

            @pl.when(here((side, dist)))
            def _():
                for p in pieces:
                    mate_copy(p, i).wait_recv()
                    if dist < line - 1:
                        @pl.when(fed)
                        def _():
                            running[p, i] = (
                                own_part[p, i]
                                + from_mate[p, i].astype(F32)
                                + run_wait(p, side, dist)
                            ).astype(BF16)

                        @pl.when(jnp.logical_not(fed))
                        def _():
                            running[p, i] = (
                                own_part[p, i] + from_mate[p, i].astype(F32)
                            ).astype(BF16)
                    else:
                        running[p, i] = (own_part[p, i] + from_mate[p, i].astype(F32)).astype(
                            BF16
                        )
                    run_copy(p, side, dist).start()

    def grp_copy(p, step):
        return pltpu.make_async_remote_copy(
            src_ref=final.at[p], dst_ref=shares_out.at[p, g],
            send_sem=grp_send.at[p, step], recv_sem=grp_recv.at[p, g],
            device_id=((g + step) % groups, f), device_id_type=MESH,
        )

    def grp_wait(p, other):
        pltpu.make_async_remote_copy(
            src_ref=final.at[p], dst_ref=shares_out.at[p, other],
            send_sem=grp_send.at[p, 0], recv_sem=grp_recv.at[p, other],
            device_id=(g, mate), device_id_type=MESH,
        ).wait_recv()

    def keep_copy(p):
        return pltpu.make_async_copy(final.at[p], shares_out.at[p, g], keep_sem.at[p])

    def finish_piece(p):
        mate_copy(p, last).wait_recv()
        own_part[p, last] += from_mate[p, last].astype(F32)

        @pl.when(has_left)
        def _():
            own_part[p, last] += run_wait(p, 1, 0)

        @pl.when(has_right)
        def _():
            own_part[p, last] += run_wait(p, -1, 0)

        final[p] = own_part[p, last].astype(BF16)
        for step in range(1, groups):
            grp_copy(p, step).start()
        keep_copy(p).start()

    load_a.wait()
    wd[f] = jnp.concatenate([a_f32[u].astype(BF16) for u in used], axis=0)
    pl.semaphore_wait(
        barrier, groups + jnp.where(has_left, 1, 0) + jnp.where(has_right, 1, 0)
    )
    gather_own(0)
    load_b.wait()
    for half in range(2):
        maps[1 + half][f] = jnp.concatenate(
            [b_f32[u, :, half * wp:(half + 1) * wp].astype(BF16) for u in used], axis=0
        )
    @pl.when(at_end)
    def _():
        gather_own(1)
        gather_own(2)

    for s in range(shards):
        load_tok(s).start()
    for s in range(shards):
        load_cot(s).start()
    acc[...] = jnp.zeros_like(acc)
    gather_span(0, 0, 2)
    pl.when(jnp.logical_not(at_end))(lambda: gather_own(1))
    gather_span(0, 2, 4 * line)
    pl.when(jnp.logical_not(at_end))(lambda: gather_own(2))
    for s in range(shards):
        load_tok(s).wait()
    accumulate(0)
    low = masked(acc[...])
    low_out[...] = low.astype(BF16)
    left_t[...] = low.T.astype(BF16)
    for s in range(shards):
        load_cot(s).wait()
    partials((0, 1), cot)
    pl.when(at_end)(lambda: pass_on((0, 1)))

    acc[...] = jnp.zeros_like(acc)
    gather_span(1, 0, 4 * line)
    pl.when(at_end)(lambda: accumulate(1))
    gather_span(2, 0, 4 * line)

    @pl.when(jnp.logical_not(at_end))
    def _():
        pass_on((0, 1))
        accumulate(1)

    accumulate(2)
    back = masked(acc[...])
    back_out[...] = back.astype(BF16)
    left_t[...] = back.T.astype(BF16)
    partials((2,), tok)
    pl.when(at_end)(lambda: pass_on((2,)))

    store_d = pltpu.make_async_copy(wd, wd_out, store_sem.at[0])
    store_l = pltpu.make_async_copy(wu_low, wu_out.at[0], store_sem.at[1])
    store_h = pltpu.make_async_copy(wu_high, wu_out.at[1], store_sem.at[2])
    store_d.start()
    store_l.start()
    store_h.start()

    finish_piece(0)
    finish_piece(1)
    pl.when(jnp.logical_not(at_end))(lambda: pass_on((2,)))

    names = [
        used_adapters(bm, other * group_blocks, group_blocks, adapters - 1)
        for other in range(groups)
    ]
    owned = [jnp.int32(-1)] * OWN_MAX
    position = jnp.int32(0)
    for a in range(adapters):
        mine = owners[a] == g
        for k in range(OWN_MAX):
            owned[k] = jnp.where(mine & (position == k), a, owned[k])
        position = position + jnp.where(mine, 1, 0)

    def count(i, totals):
        entry = bm[i]
        return tuple(n + jnp.where(entry == o, 1, 0) for n, o in zip(totals, owned))

    totals = lax.fori_loop(0, total_blocks, count, (jnp.int32(0),) * OWN_MAX, unroll=8)
    shape = (OWN_MAX * RANK, groups * ROWS)
    row = lax.broadcasted_iota(jnp.int32, shape, 0)
    col = lax.broadcasted_iota(jnp.int32, shape, 1)
    row_name = jnp.full(shape, -1, jnp.int32)
    col_name = jnp.full(shape, -2, jnp.int32)
    for k in range(OWN_MAX):
        row_name = jnp.where(row // RANK == k, owned[k], row_name)
    for q in range(groups * USED):
        col_name = jnp.where(col // RANK == q, names[q // USED][q % USED], col_name)
    hit = (row % RANK == col % RANK) & (row_name == col_name)
    pick_out[...] = jnp.where(hit, 1.0, 0.0).astype(BF16)
    wide = lax.broadcasted_iota(jnp.int32, scale_out.shape, 0) // RANK
    uses = jnp.zeros(scale_out.shape, jnp.int32)
    for k in range(OWN_MAX):
        uses = jnp.where(wide == k, totals[k], uses)
    scale_out[...] = 1.0 / (BLOCK * jnp.maximum(uses, 1)).astype(F32)

    finish_piece(2)
    for piece in range(PIECES):
        gather_finish(piece)

    for i, step in enumerate(steps):
        @pl.when(here(step))
        def _():
            for p in range(PIECES):
                mate_copy(p, i).wait_send()
                if i != last:
                    run_copy(p, *step).wait_send()

    store_d.wait()
    store_l.wait()
    store_h.wait()
    for p in range(PIECES):
        keep_copy(p).wait()
        for step in range(1, groups):
            grp_copy(p, step).wait_send()
        for step in range(1, groups):
            grp_wait(p, (g + step) % groups)


def outputs(
    low, back, pick, scale, wd, wu, up_shares, down_shares,
    delta, grad_tokens, grad_down, grad_up,
):
    count, _, wp = wd.shape
    for s in range(count):
        for half in range(2):
            start = (s * 2 + half) * wp
            delta[:, start:start + wp] = jnp.dot(
                low[...], wu[half, s], preferred_element_type=F32
            ).astype(delta.dtype)
        grad_tokens[:, s * wp:(s + 1) * wp] = jnp.dot(
            back[...], wd[s], preferred_element_type=F32
        ).astype(grad_tokens.dtype)
    for shares, grad in ((down_shares, grad_down), (up_shares, grad_up)):
        total = jnp.dot(pick[...], shares[0], preferred_element_type=F32)
        grad[...] = (total * scale[:, 0:1]).reshape(grad.shape)


def on_device(groups, shards, tokens, cotangent, adapter_a, adapter_b, block_map, adapter_owner):
    rows, width = tokens.shape
    hidden = cotangent.shape[1]
    wp = adapter_a.shape[2]
    assert adapter_b.shape[2] == 2 * wp
    line = shards // 2
    dma = pltpu.SemaphoreType.DMA
    vmem = pl.BlockSpec(memory_space=pltpu.VMEM)
    smem = pl.BlockSpec(memory_space=pltpu.SMEM)
    anywhere = pl.BlockSpec(memory_space=pl.ANY)
    low, back, pick, scale, wd, wu, shares = pl.pallas_call(
        functools.partial(exchange, groups, shards),
        name="exchange",
        out_shape=(
            jax.ShapeDtypeStruct((rows, ROWS), BF16),
            jax.ShapeDtypeStruct((rows, ROWS), BF16),
            jax.ShapeDtypeStruct((OWN_MAX * RANK, groups * ROWS), BF16),
            jax.ShapeDtypeStruct((OWN_MAX * RANK, 128), F32),
            jax.ShapeDtypeStruct((shards, ROWS, wp), BF16),
            jax.ShapeDtypeStruct((2, shards, ROWS, wp), BF16),
            jax.ShapeDtypeStruct((PIECES, groups, ROWS, wp), BF16),
        ),
        in_specs=[smem, smem] + [anywhere] * 4,
        out_specs=(vmem,) * 4 + (anywhere,) * 3,
        scratch_shapes=[
            pltpu.VMEM(adapter_a.shape, F32),
            pltpu.VMEM(adapter_b.shape, F32),
            pltpu.VMEM((shards, ROWS, wp), BF16),
            pltpu.VMEM((shards, ROWS, wp), BF16),
            pltpu.VMEM((shards, ROWS, wp), BF16),
            pltpu.VMEM((shards, rows, wp), BF16),
            pltpu.VMEM((shards, rows, 2 * wp), BF16),
            pltpu.VMEM((rows, ROWS), F32),
            pltpu.VMEM((ROWS, rows), BF16),
            pltpu.VMEM((PIECES, 2 * line - 1, ROWS, wp), BF16),
            pltpu.VMEM((PIECES, 2 * line - 1, ROWS, wp), BF16),
            pltpu.VMEM((PIECES, 2 * line - 1, ROWS, wp), F32),
            pltpu.VMEM((PIECES, 2, line, ROWS, wp), BF16),
            pltpu.VMEM((PIECES, 2 * line - 1, ROWS, wp), BF16),
            pltpu.VMEM((PIECES, ROWS, wp), BF16),
            dma((2,)),
            dma((shards,)),
            dma((shards,)),
            dma((3,)),
            dma((3, PIECES, line)),
            dma((PIECES, shards)),
            dma((PIECES, 2 * line - 1)),
            dma((PIECES, 2 * line - 1)),
            dma((PIECES, 2 * line - 1)),
            dma((PIECES, 2, line)),
            dma((PIECES, groups)),
            dma((PIECES, groups)),
            dma((PIECES,)),
        ],
        compiler_params=pltpu.CompilerParams(
            collective_id=0, has_side_effects=True, vmem_limit_bytes=56 * 1024 * 1024
        ),
    )(block_map, adapter_owner, adapter_a, adapter_b, tokens, cotangent)
    shares = shares.reshape(PIECES, groups * ROWS, wp)
    steps = min(4, wp // 128)
    half = steps // 2
    whole = lambda shape: pl.BlockSpec(shape, lambda i: (0,) * len(shape))
    return pl.pallas_call(
        outputs,
        name="outputs",
        grid=(steps,),
        out_shape=(
            jax.ShapeDtypeStruct((rows, hidden), BF16),
            jax.ShapeDtypeStruct((rows, width), BF16),
            jax.ShapeDtypeStruct((OWN_MAX, RANK, wp), F32),
            jax.ShapeDtypeStruct((OWN_MAX, RANK, 2 * wp), F32),
        ),
        in_specs=[
            whole(low.shape), whole(back.shape), whole(pick.shape), whole(scale.shape),
            pl.BlockSpec((shards // steps, ROWS, wp), lambda i: (i, 0, 0)),
            pl.BlockSpec((2, shards // steps, ROWS, wp), lambda i: (0, i, 0, 0)),
            pl.BlockSpec((1, groups * ROWS, wp // half), lambda i: (i // half, 0, i % half)),
            pl.BlockSpec((1, groups * ROWS, wp // steps), lambda i: (2, 0, i)),
        ],
        out_specs=(
            pl.BlockSpec((rows, hidden // steps), lambda i: (0, i)),
            pl.BlockSpec((rows, width // steps), lambda i: (0, i)),
            pl.BlockSpec((OWN_MAX, RANK, wp // steps), lambda i: (0, 0, i)),
            pl.BlockSpec((OWN_MAX, RANK, 2 * wp // steps), lambda i: (0, 0, i)),
        ),
    )(low, back, pick, scale, wd, wu, shares, shares)


def solution(mesh):
    placed = (
        P(("grp", "fsdp"), None),
        P(("grp", "fsdp"), None),
        P(None, None, "fsdp"),
        P(None, None, "fsdp"),
        P(),
        P(),
    )
    return jax.shard_map(
        functools.partial(on_device, mesh.shape["grp"], mesh.shape["fsdp"]),
        mesh=mesh,
        in_specs=placed,
        out_specs=(
            P(("grp", "fsdp"), None),
            P(("grp", "fsdp"), None),
            P("grp", None, "fsdp"),
            P("grp", None, "fsdp"),
        ),
        check_vma=False,
    )
```

```python
import functools

import jax
import jax.numpy as jnp
from jax import lax
from jax.experimental import pallas as pl
from jax.experimental.pallas import tpu as pltpu
from jax.sharding import PartitionSpec as P

BLOCK = 128
USED = 4
OWN_MAX = 8
RANK = 16
ROWS = USED * RANK
MESH = pl.DeviceIdType.MESH
NT = (((1,), (1,)), ((), ()))
PIECES = 3
RIGHT, LEFT, PARTNER = 0, 1, 2
BF16, F32 = jnp.bfloat16, jnp.float32


def used_adapters(bm, base, count, last_name):
    found = []
    for _ in range(USED):
        def smallest(i, best, last=found[-1] if found else -1):
            entry = bm[base + i]
            return jnp.where((entry > last) & (entry < best), entry, best)

        found.append(lax.fori_loop(0, count, smallest, jnp.int32(last_name), unroll=min(count, 16)))
    return found


def exchange(
    groups, shards,
    bm, owners, a_hbm, b_hbm, tokens, cotangent,
    low_out, back_out, pick_out, scale_out, wd_out, wu_out, shares_out,
    a_f32, b_f32, wd, wu_low, wu_high, tok, cot, acc, left_t,
    to_mate, from_mate, own_part, arrived, running, final,
    load_sem, tok_sem, cot_sem, store_sem, ag_send, ag_recv,
    mate_send, mate_recv, run_send, run_recv, grp_send, grp_recv, keep_sem,
):
    line = shards // 2
    g = lax.axis_index("grp")
    f = lax.axis_index("fsdp")
    z = f // 2
    c = f % 2
    mate = z * 2 + (1 - c)
    wp = a_hbm.shape[2]
    rows = tokens.shape[0]
    blocks_dev = rows // BLOCK
    total_blocks = bm.shape[0]
    group_blocks = total_blocks // groups
    adapters = a_hbm.shape[0]
    has_left, has_right = z > 0, z < line - 1
    at_end = (z == 0) | (z == line - 1)

    maps = (wd, wu_low, wu_high)

    barrier = pltpu.get_barrier_semaphore()

    def greet(target):
        pl.semaphore_signal(barrier, inc=1, device_id=target, device_id_type=MESH)

    greet((g, mate))
    pl.when(has_left)(lambda: greet((g, f - 2)))
    pl.when(has_right)(lambda: greet((g, f + 2)))
    for step in range(1, groups):
        greet(((g + step) % groups, f))

    load_a = pltpu.make_async_copy(a_hbm, a_f32, load_sem.at[0])
    load_b = pltpu.make_async_copy(b_hbm, b_f32, load_sem.at[1])
    load_a.start()
    load_b.start()

    def load_tok(s):
        return pltpu.make_async_copy(
            tokens.at[:, pl.ds(pl.multiple_of(s * wp, 128), wp)], tok.at[s], tok_sem.at[s]
        )

    def load_cot(s):
        return pltpu.make_async_copy(
            cotangent.at[:, pl.ds(pl.multiple_of(s * 2 * wp, 128), 2 * wp)], cot.at[s], cot_sem.at[s]
        )

    used = used_adapters(bm, g * group_blocks, group_blocks, adapters - 1)

    def weights(piece, shard):
        return maps[piece].at[shard]

    def gather_copy(piece, origin, way):
        ref = weights(piece, origin)
        target = {RIGHT: f + 2, LEFT: f - 2, PARTNER: mate}[way]
        return pltpu.make_async_remote_copy(
            src_ref=ref, dst_ref=ref,
            send_sem=ag_send.at[way, piece, origin // 2],
            recv_sem=ag_recv.at[piece, origin],
            device_id=(g, target), device_id_type=MESH,
        )

    def gather_own(piece):
        pl.when(has_right)(lambda: gather_copy(piece, f, RIGHT).start())
        pl.when(has_left)(lambda: gather_copy(piece, f, LEFT).start())
        gather_copy(piece, f, PARTNER).start()

    def accumulate(piece):
        def body(s, _):
            if piece == 0:
                values = tok[s]
            else:
                values = cot[s, :, (piece - 1) * wp:piece * wp]
            acc[...] += lax.dot_general(values, maps[piece][s], NT, preferred_element_type=F32)
            return 0

        lax.fori_loop(0, shards, body, 0, unroll=4)

    def gather_span(piece, first, last):
        def body(q, _):
            same = 1 - (q % 4) // 2
            side = 2 * (q % 2) - 1
            dist = q // 4 + same
            place = z + side * dist
            here = (place >= 0) & (place < line) & ((side < 0) | (dist > 0))
            origin = place * 2 + (c + 1 - same) % 2

            @pl.when(here)
            def _():
                gather_copy(piece, origin, PARTNER).wait_recv()

                @pl.when((same == 1) & (side < 0) & has_right)
                def _():
                    gather_copy(piece, origin, RIGHT).start()

                @pl.when((same == 1) & (side > 0) & has_left)
                def _():
                    gather_copy(piece, origin, LEFT).start()

                @pl.when(same == 1)
                def _():
                    gather_copy(piece, origin, PARTNER).start()

            return 0

        lax.fori_loop(first, last, body, 0)

    def gather_finish(piece):
        def body(place, _):
            origin = place * 2 + c
            pl.when((place <= z) & has_right)(
                lambda: gather_copy(piece, origin, RIGHT).wait_send()
            )
            pl.when((place >= z) & has_left)(
                lambda: gather_copy(piece, origin, LEFT).wait_send()
            )
            gather_copy(piece, origin, PARTNER).wait_send()
            return 0

        lax.fori_loop(0, line, body, 0)

    def masked(total):
        row = lax.broadcasted_iota(jnp.int32, (rows, ROWS), 0) // BLOCK
        slot = lax.broadcasted_iota(jnp.int32, (rows, ROWS), 1) // RANK
        wanted = jnp.zeros((rows, ROWS), jnp.int32)
        for b in range(blocks_dev):
            entry = bm[(g * shards + f) * blocks_dev + b]
            place = jnp.int32(0)
            for s in range(1, USED):
                place = jnp.where(entry == used[s], s, place)
            wanted = jnp.where(row == b, place, wanted)
        return jnp.where(slot == wanted, total, 0.0)

    steps = [(side, dist) for dist in range(line - 1, 0, -1) for side in (1, -1)] + [(1, 0)]
    number = {step: i for i, step in enumerate(steps)}
    last = number[(1, 0)]

    def here(step):
        side, dist = step
        return z + dist < line if side > 0 else z - dist >= 0

    def mate_copy(p, i):
        return pltpu.make_async_remote_copy(
            src_ref=to_mate.at[p, i], dst_ref=from_mate.at[p, i],
            send_sem=mate_send.at[p, i], recv_sem=mate_recv.at[p, i],
            device_id=(g, mate), device_id_type=MESH,
        )

    def partial_step(pieces, values, i):
        side, dist = steps[i]
        d = z + side * dist

        @pl.when(here((side, dist)))
        def _():
            given = jnp.dot(left_t[...], values[d * 2 + (1 - c)], preferred_element_type=F32)
            for n, p in enumerate(pieces):
                to_mate[p, i] = given[:, n * wp:(n + 1) * wp].astype(BF16)
            for p in pieces:
                mate_copy(p, i).start()
            kept = jnp.dot(left_t[...], values[d * 2 + c], preferred_element_type=F32)
            for n, p in enumerate(pieces):
                own_part[p, i] = kept[:, n * wp:(n + 1) * wp]

    def run_copy(p, side, dist):
        row = (1 - side) // 2
        return pltpu.make_async_remote_copy(
            src_ref=running.at[p, number[(side, dist)]], dst_ref=arrived.at[p, row, dist - 1],
            send_sem=run_send.at[p, number[(side, dist)]], recv_sem=run_recv.at[p, row, dist - 1],
            device_id=(g, f + 2 * side), device_id_type=MESH,
        )

    def run_wait(p, side, dist):
        run_copy(p, side, dist + 1).wait_recv()
        return arrived[p, (1 - side) // 2, dist].astype(F32)

    def pass_step(pieces, i):
        side, dist = steps[i]
        fed = has_left if side > 0 else has_right

        @pl.when(here((side, dist)))
        def _():
            for p in pieces:
                mate_copy(p, i).wait_recv()
                if dist < line - 1:
                    @pl.when(fed)
                    def _():
                        running[p, i] = (
                            own_part[p, i]
                            + from_mate[p, i].astype(F32)
                            + run_wait(p, side, dist)
                        ).astype(BF16)

                    @pl.when(jnp.logical_not(fed))
                    def _():
                        running[p, i] = (own_part[p, i] + from_mate[p, i].astype(F32)).astype(
                            BF16
                        )
                else:
                    running[p, i] = (own_part[p, i] + from_mate[p, i].astype(F32)).astype(BF16)
                run_copy(p, side, dist).start()

    def pass_on(pieces):
        for i in range(last):
            pass_step(pieces, i)

    def partials(pieces, values):
        for i in range(len(steps)):
            partial_step(pieces, values, i)
            if i >= 2:
                pl.when(at_end)(lambda: pass_step(pieces, i - 2))
        pl.when(at_end)(lambda: pass_step(pieces, last - 1))

    beside, across = g + 1 - 2 * (g % 2), (g + 2) % groups

    def half_of(ref, half):
        return ref.at[pl.ds(half * (ROWS // 2), ROWS // 2)]

    def grp_copy(p, n):
        near, half, far = ((beside, 0, g), (beside, 1, g), (across, 0, g), (across, 1, g),
                           (across, 0, beside), (beside, 1, across))[n]
        place = half_of(shares_out.at[p, far], half)
        return pltpu.make_async_remote_copy(
            src_ref=half_of(final.at[p], half) if n < 4 else place, dst_ref=place,
            send_sem=grp_send.at[p, n], recv_sem=grp_recv.at[p, n],
            device_id=(near, f), device_id_type=MESH,
        )

    def grp_wait(p, n):
        far, half = ((beside, 0), (beside, 1), (across, 0), (across, 1),
                     (groups - 1 - g, 0), (groups - 1 - g, 1))[n]
        place = half_of(shares_out.at[p, far], half)
        pltpu.make_async_remote_copy(
            src_ref=place, dst_ref=place,
            send_sem=grp_send.at[p, n], recv_sem=grp_recv.at[p, n],
            device_id=(beside, f), device_id_type=MESH,
        ).wait_recv()

    def relay(p):
        grp_wait(p, 0)
        grp_copy(p, 4).start()
        grp_wait(p, 3)
        grp_copy(p, 5).start()

    def keep_copy(p):
        return pltpu.make_async_copy(final.at[p], shares_out.at[p, g], keep_sem.at[p])

    def finish_piece(p):
        mate_copy(p, last).wait_recv()
        own_part[p, last] += from_mate[p, last].astype(F32)

        @pl.when(has_left)
        def _():
            own_part[p, last] += run_wait(p, 1, 0)

        @pl.when(has_right)
        def _():
            own_part[p, last] += run_wait(p, -1, 0)

        final[p] = own_part[p, last].astype(BF16)
        for n in (0, 3, 1, 2):
            grp_copy(p, n).start()
        keep_copy(p).start()

    load_a.wait()
    wd[f] = jnp.concatenate([a_f32[u].astype(BF16) for u in used], axis=0)
    pl.semaphore_wait(
        barrier, groups + jnp.where(has_left, 1, 0) + jnp.where(has_right, 1, 0)
    )
    gather_own(0)
    load_b.wait()
    for half in range(2):
        maps[1 + half][f] = jnp.concatenate(
            [b_f32[u, :, half * wp:(half + 1) * wp].astype(BF16) for u in used], axis=0
        )
    @pl.when(at_end)
    def _():
        gather_own(1)
        gather_own(2)

    for s in range(shards):
        load_tok(s).start()
    for s in range(shards):
        load_cot(s).start()
    acc[...] = jnp.zeros_like(acc)
    gather_span(0, 0, 2)
    pl.when(jnp.logical_not(at_end))(lambda: gather_own(1))
    gather_span(0, 2, 4 * line)
    pl.when(jnp.logical_not(at_end))(lambda: gather_own(2))
    for s in range(shards):
        load_tok(s).wait()
    accumulate(0)
    low = masked(acc[...])
    low_out[...] = low.astype(BF16)
    left_t[...] = low.T.astype(BF16)
    for s in range(shards):
        load_cot(s).wait()
    partials((0, 1), cot)

    acc[...] = jnp.zeros_like(acc)
    gather_span(1, 0, 4 * line)
    pl.when(at_end)(lambda: accumulate(1))
    gather_span(2, 0, 4 * line)

    @pl.when(jnp.logical_not(at_end))
    def _():
        pass_on((0, 1))
        accumulate(1)

    accumulate(2)
    back = masked(acc[...])
    back_out[...] = back.astype(BF16)
    left_t[...] = back.T.astype(BF16)
    partials((2,), tok)

    store_d = pltpu.make_async_copy(wd, wd_out, store_sem.at[0])
    store_l = pltpu.make_async_copy(wu_low, wu_out.at[0], store_sem.at[1])
    store_h = pltpu.make_async_copy(wu_high, wu_out.at[1], store_sem.at[2])
    store_d.start()
    store_l.start()
    store_h.start()

    finish_piece(0)
    finish_piece(1)
    relay(0)
    pl.when(jnp.logical_not(at_end))(lambda: pass_on((2,)))

    names = [
        used_adapters(bm, other * group_blocks, group_blocks, adapters - 1)
        for other in range(groups)
    ]
    owned = [jnp.int32(-1)] * OWN_MAX
    position = jnp.int32(0)
    for a in range(adapters):
        mine = owners[a] == g
        for k in range(OWN_MAX):
            owned[k] = jnp.where(mine & (position == k), a, owned[k])
        position = position + jnp.where(mine, 1, 0)

    def count(i, totals):
        entry = bm[i]
        return tuple(n + jnp.where(entry == o, 1, 0) for n, o in zip(totals, owned))

    totals = lax.fori_loop(0, total_blocks, count, (jnp.int32(0),) * OWN_MAX, unroll=8)
    shape = (OWN_MAX * RANK, groups * ROWS)
    row = lax.broadcasted_iota(jnp.int32, shape, 0)
    col = lax.broadcasted_iota(jnp.int32, shape, 1)
    row_name = jnp.full(shape, -1, jnp.int32)
    col_name = jnp.full(shape, -2, jnp.int32)
    for k in range(OWN_MAX):
        row_name = jnp.where(row // RANK == k, owned[k], row_name)
    for q in range(groups * USED):
        col_name = jnp.where(col // RANK == q, names[q // USED][q % USED], col_name)
    hit = (row % RANK == col % RANK) & (row_name == col_name)
    pick_out[...] = jnp.where(hit, 1.0, 0.0).astype(BF16)
    wide = lax.broadcasted_iota(jnp.int32, scale_out.shape, 0) // RANK
    uses = jnp.zeros(scale_out.shape, jnp.int32)
    for k in range(OWN_MAX):
        uses = jnp.where(wide == k, totals[k], uses)
    scale_out[...] = 1.0 / (BLOCK * jnp.maximum(uses, 1)).astype(F32)

    relay(1)
    finish_piece(2)
    relay(2)
    for piece in range(PIECES):
        gather_finish(piece)

    for i, step in enumerate(steps):
        @pl.when(here(step))
        def _():
            for p in range(PIECES):
                mate_copy(p, i).wait_send()
                if i != last:
                    run_copy(p, *step).wait_send()

    store_d.wait()
    store_l.wait()
    store_h.wait()
    for p in range(PIECES):
        keep_copy(p).wait()
        for n in range(6):
            grp_copy(p, n).wait_send()
        for n in (1, 2, 4, 5):
            grp_wait(p, n)


def outputs(
    low, back, pick, scale, wd, wu, up_shares, down_shares,
    delta, grad_tokens, grad_down, grad_up,
):
    count, _, wp = wd.shape
    for s in range(count):
        for half in range(2):
            start = (s * 2 + half) * wp
            delta[:, start:start + wp] = jnp.dot(
                low[...], wu[half, s], preferred_element_type=F32
            ).astype(delta.dtype)
        grad_tokens[:, s * wp:(s + 1) * wp] = jnp.dot(
            back[...], wd[s], preferred_element_type=F32
        ).astype(grad_tokens.dtype)
    for shares, grad in ((down_shares, grad_down), (up_shares, grad_up)):
        total = jnp.dot(pick[...], shares[0], preferred_element_type=F32)
        grad[...] = (total * scale[:, 0:1]).reshape(grad.shape)


def on_device(groups, shards, tokens, cotangent, adapter_a, adapter_b, block_map, adapter_owner):
    rows, width = tokens.shape
    hidden = cotangent.shape[1]
    wp = adapter_a.shape[2]
    assert adapter_b.shape[2] == 2 * wp
    line = shards // 2
    assert groups == 4
    dma = pltpu.SemaphoreType.DMA
    vmem = pl.BlockSpec(memory_space=pltpu.VMEM)
    smem = pl.BlockSpec(memory_space=pltpu.SMEM)
    anywhere = pl.BlockSpec(memory_space=pl.ANY)
    low, back, pick, scale, wd, wu, shares = pl.pallas_call(
        functools.partial(exchange, groups, shards),
        name="exchange",
        out_shape=(
            jax.ShapeDtypeStruct((rows, ROWS), BF16),
            jax.ShapeDtypeStruct((rows, ROWS), BF16),
            jax.ShapeDtypeStruct((OWN_MAX * RANK, groups * ROWS), BF16),
            jax.ShapeDtypeStruct((OWN_MAX * RANK, 128), F32),
            jax.ShapeDtypeStruct((shards, ROWS, wp), BF16),
            jax.ShapeDtypeStruct((2, shards, ROWS, wp), BF16),
            jax.ShapeDtypeStruct((PIECES, groups, ROWS, wp), BF16),
        ),
        in_specs=[smem, smem] + [anywhere] * 4,
        out_specs=(vmem,) * 4 + (anywhere,) * 3,
        scratch_shapes=[
            pltpu.VMEM(adapter_a.shape, F32),
            pltpu.VMEM(adapter_b.shape, F32),
            pltpu.VMEM((shards, ROWS, wp), BF16),
            pltpu.VMEM((shards, ROWS, wp), BF16),
            pltpu.VMEM((shards, ROWS, wp), BF16),
            pltpu.VMEM((shards, rows, wp), BF16),
            pltpu.VMEM((shards, rows, 2 * wp), BF16),
            pltpu.VMEM((rows, ROWS), F32),
            pltpu.VMEM((ROWS, rows), BF16),
            pltpu.VMEM((PIECES, 2 * line - 1, ROWS, wp), BF16),
            pltpu.VMEM((PIECES, 2 * line - 1, ROWS, wp), BF16),
            pltpu.VMEM((PIECES, 2 * line - 1, ROWS, wp), F32),
            pltpu.VMEM((PIECES, 2, line, ROWS, wp), BF16),
            pltpu.VMEM((PIECES, 2 * line - 1, ROWS, wp), BF16),
            pltpu.VMEM((PIECES, ROWS, wp), BF16),
            dma((2,)),
            dma((shards,)),
            dma((shards,)),
            dma((3,)),
            dma((3, PIECES, line)),
            dma((PIECES, shards)),
            dma((PIECES, 2 * line - 1)),
            dma((PIECES, 2 * line - 1)),
            dma((PIECES, 2 * line - 1)),
            dma((PIECES, 2, line)),
            dma((PIECES, 6)),
            dma((PIECES, 6)),
            dma((PIECES,)),
        ],
        compiler_params=pltpu.CompilerParams(
            collective_id=0, has_side_effects=True, vmem_limit_bytes=56 * 1024 * 1024
        ),
    )(block_map, adapter_owner, adapter_a, adapter_b, tokens, cotangent)
    shares = shares.reshape(PIECES, groups * ROWS, wp)
    steps = min(4, wp // 128)
    half = steps // 2
    whole = lambda shape: pl.BlockSpec(shape, lambda i: (0,) * len(shape))
    return pl.pallas_call(
        outputs,
        name="outputs",
        grid=(steps,),
        out_shape=(
            jax.ShapeDtypeStruct((rows, hidden), BF16),
            jax.ShapeDtypeStruct((rows, width), BF16),
            jax.ShapeDtypeStruct((OWN_MAX, RANK, wp), F32),
            jax.ShapeDtypeStruct((OWN_MAX, RANK, 2 * wp), F32),
        ),
        in_specs=[
            whole(low.shape), whole(back.shape), whole(pick.shape), whole(scale.shape),
            pl.BlockSpec((shards // steps, ROWS, wp), lambda i: (i, 0, 0)),
            pl.BlockSpec((2, shards // steps, ROWS, wp), lambda i: (0, i, 0, 0)),
            pl.BlockSpec((1, groups * ROWS, wp // half), lambda i: (i // half, 0, i % half)),
            pl.BlockSpec((1, groups * ROWS, wp // steps), lambda i: (2, 0, i)),
        ],
        out_specs=(
            pl.BlockSpec((rows, hidden // steps), lambda i: (0, i)),
            pl.BlockSpec((rows, width // steps), lambda i: (0, i)),
            pl.BlockSpec((OWN_MAX, RANK, wp // steps), lambda i: (0, 0, i)),
            pl.BlockSpec((OWN_MAX, RANK, 2 * wp // steps), lambda i: (0, 0, i)),
        ),
    )(low, back, pick, scale, wd, wu, shares, shares)


def solution(mesh):
    placed = (
        P(("grp", "fsdp"), None),
        P(("grp", "fsdp"), None),
        P(None, None, "fsdp"),
        P(None, None, "fsdp"),
        P(),
        P(),
    )
    return jax.shard_map(
        functools.partial(on_device, mesh.shape["grp"], mesh.shape["fsdp"]),
        mesh=mesh,
        in_specs=placed,
        out_specs=(
            P(("grp", "fsdp"), None),
            P(("grp", "fsdp"), None),
            P("grp", None, "fsdp"),
            P("grp", None, "fsdp"),
        ),
        check_vma=False,
    )
```

```python
import functools

import jax
import jax.numpy as jnp
from jax import lax
from jax.experimental import pallas as pl
from jax.experimental.pallas import tpu as pltpu
from jax.sharding import PartitionSpec as P

BLOCK = 128
USED = 4
OWN_MAX = 8
RANK = 16
ROWS = USED * RANK
MESH = pl.DeviceIdType.MESH
NT = (((1,), (1,)), ((), ()))
PIECES = 3
RIGHT, LEFT, PARTNER = 0, 1, 2
BF16, F32 = jnp.bfloat16, jnp.float32


def used_adapters(bm, base, count, last_name):
    found = []
    for _ in range(USED):
        def smallest(i, best, last=found[-1] if found else -1):
            entry = bm[base + i]
            return jnp.where((entry > last) & (entry < best), entry, best)

        found.append(lax.fori_loop(0, count, smallest, jnp.int32(last_name), unroll=min(count, 16)))
    return found


def exchange(
    groups, shards,
    bm, owners, a_hbm, b_hbm, tokens, cotangent,
    low_out, back_out, pick_out, scale_out, wd_out, wu_out, shares_out,
    a_f32, b_f32, wd, wu_low, wu_high, tok, cot, acc, left_t,
    to_mate, from_mate, own_part, arrived, running, final,
    load_sem, tok_sem, cot_sem, store_sem, ag_send, ag_recv,
    mate_send, mate_recv, run_send, run_recv, grp_send, grp_recv, keep_sem,
):
    line = shards // 2
    g = lax.axis_index("grp")
    f = lax.axis_index("fsdp")
    z = f // 2
    c = f % 2
    mate = z * 2 + (1 - c)
    wp = a_hbm.shape[2]
    rows = tokens.shape[0]
    blocks_dev = rows // BLOCK
    total_blocks = bm.shape[0]
    group_blocks = total_blocks // groups
    adapters = a_hbm.shape[0]
    has_left, has_right = z > 0, z < line - 1
    at_end = (z == 0) | (z == line - 1)

    maps = (wd, wu_low, wu_high)

    barrier = pltpu.get_barrier_semaphore()

    def greet(target):
        pl.semaphore_signal(barrier, inc=1, device_id=target, device_id_type=MESH)

    greet((g, mate))
    pl.when(has_left)(lambda: greet((g, f - 2)))
    pl.when(has_right)(lambda: greet((g, f + 2)))
    for step in range(1, groups):
        greet(((g + step) % groups, f))

    load_a = pltpu.make_async_copy(a_hbm, a_f32, load_sem.at[0])
    load_b = pltpu.make_async_copy(b_hbm, b_f32, load_sem.at[1])
    load_a.start()
    load_b.start()

    def load_tok(s):
        return pltpu.make_async_copy(
            tokens.at[:, pl.ds(pl.multiple_of(s * wp, 128), wp)], tok.at[s], tok_sem.at[s]
        )

    def load_cot(s):
        return pltpu.make_async_copy(
            cotangent.at[:, pl.ds(pl.multiple_of(s * 2 * wp, 128), 2 * wp)], cot.at[s], cot_sem.at[s]
        )

    used = used_adapters(bm, g * group_blocks, group_blocks, adapters - 1)

    def weights(piece, shard):
        return maps[piece].at[shard]

    def gather_copy(piece, origin, way):
        ref = weights(piece, origin)
        target = {RIGHT: f + 2, LEFT: f - 2, PARTNER: mate}[way]
        return pltpu.make_async_remote_copy(
            src_ref=ref, dst_ref=ref,
            send_sem=ag_send.at[way, piece, origin // 2],
            recv_sem=ag_recv.at[piece, origin],
            device_id=(g, target), device_id_type=MESH,
        )

    def gather_own(piece):
        pl.when(has_right)(lambda: gather_copy(piece, f, RIGHT).start())
        pl.when(has_left)(lambda: gather_copy(piece, f, LEFT).start())
        gather_copy(piece, f, PARTNER).start()

    def accumulate(piece):
        def body(s, _):
            if piece == 0:
                values = tok[s]
            else:
                values = cot[s, :, (piece - 1) * wp:piece * wp]
            acc[...] += lax.dot_general(values, maps[piece][s], NT, preferred_element_type=F32)
            return 0

        lax.fori_loop(0, shards, body, 0, unroll=4)

    def gather_span(piece, first, last):
        def body(q, _):
            same = 1 - (q % 4) // 2
            side = 2 * (q % 2) - 1
            dist = q // 4 + same
            place = z + side * dist
            here = (place >= 0) & (place < line) & ((side < 0) | (dist > 0))
            origin = place * 2 + (c + 1 - same) % 2

            @pl.when(here)
            def _():
                gather_copy(piece, origin, PARTNER).wait_recv()

                @pl.when((same == 1) & (side < 0) & has_right)
                def _():
                    gather_copy(piece, origin, RIGHT).start()

                @pl.when((same == 1) & (side > 0) & has_left)
                def _():
                    gather_copy(piece, origin, LEFT).start()

                @pl.when(same == 1)
                def _():
                    gather_copy(piece, origin, PARTNER).start()

            return 0

        lax.fori_loop(first, last, body, 0)

    def gather_finish(piece):
        def body(place, _):
            origin = place * 2 + c
            pl.when((place <= z) & has_right)(
                lambda: gather_copy(piece, origin, RIGHT).wait_send()
            )
            pl.when((place >= z) & has_left)(
                lambda: gather_copy(piece, origin, LEFT).wait_send()
            )
            gather_copy(piece, origin, PARTNER).wait_send()
            return 0

        lax.fori_loop(0, line, body, 0)

    def masked(total):
        row = lax.broadcasted_iota(jnp.int32, (rows, ROWS), 0) // BLOCK
        slot = lax.broadcasted_iota(jnp.int32, (rows, ROWS), 1) // RANK
        wanted = jnp.zeros((rows, ROWS), jnp.int32)
        for b in range(blocks_dev):
            entry = bm[(g * shards + f) * blocks_dev + b]
            place = jnp.int32(0)
            for s in range(1, USED):
                place = jnp.where(entry == used[s], s, place)
            wanted = jnp.where(row == b, place, wanted)
        return jnp.where(slot == wanted, total, 0.0)

    steps = [(side, dist) for dist in range(line - 1, 0, -1) for side in (1, -1)] + [(1, 0)]
    number = {step: i for i, step in enumerate(steps)}
    last = number[(1, 0)]

    def here(step):
        side, dist = step
        return z + dist < line if side > 0 else z - dist >= 0

    def mate_copy(p, i):
        return pltpu.make_async_remote_copy(
            src_ref=to_mate.at[p, i], dst_ref=from_mate.at[p, i],
            send_sem=mate_send.at[p, i], recv_sem=mate_recv.at[p, i],
            device_id=(g, mate), device_id_type=MESH,
        )

    def partial_step(pieces, values, i):
        side, dist = steps[i]
        d = z + side * dist

        @pl.when(here((side, dist)))
        def _():
            given = jnp.dot(left_t[...], values[d * 2 + (1 - c)], preferred_element_type=F32)
            for n, p in enumerate(pieces):
                to_mate[p, i] = given[:, n * wp:(n + 1) * wp].astype(BF16)
            for p in pieces:
                mate_copy(p, i).start()
            kept = jnp.dot(left_t[...], values[d * 2 + c], preferred_element_type=F32)
            for n, p in enumerate(pieces):
                own_part[p, i] = kept[:, n * wp:(n + 1) * wp]

    def run_copy(p, side, dist):
        row = (1 - side) // 2
        return pltpu.make_async_remote_copy(
            src_ref=running.at[p, number[(side, dist)]], dst_ref=arrived.at[p, row, dist - 1],
            send_sem=run_send.at[p, number[(side, dist)]], recv_sem=run_recv.at[p, row, dist - 1],
            device_id=(g, f + 2 * side), device_id_type=MESH,
        )

    def run_wait(p, side, dist):
        run_copy(p, side, dist + 1).wait_recv()
        return arrived[p, (1 - side) // 2, dist].astype(F32)

    def pass_step(pieces, i):
        side, dist = steps[i]
        fed = has_left if side > 0 else has_right

        @pl.when(here((side, dist)))
        def _():
            for p in pieces:
                mate_copy(p, i).wait_recv()
                if dist < line - 1:
                    @pl.when(fed)
                    def _():
                        running[p, i] = (
                            own_part[p, i]
                            + from_mate[p, i].astype(F32)
                            + run_wait(p, side, dist)
                        ).astype(BF16)

                    @pl.when(jnp.logical_not(fed))
                    def _():
                        running[p, i] = (own_part[p, i] + from_mate[p, i].astype(F32)).astype(
                            BF16
                        )
                else:
                    running[p, i] = (own_part[p, i] + from_mate[p, i].astype(F32)).astype(BF16)
                run_copy(p, side, dist).start()

    def pass_on(pieces):
        for i in range(last):
            pass_step(pieces, i)

    def partials(pieces, values):
        for i in range(len(steps)):
            partial_step(pieces, values, i)
            if i >= 2:
                pl.when(at_end)(lambda: pass_step(pieces, i - 2))
        pl.when(at_end)(lambda: pass_step(pieces, last - 1))

    def grp_copy(p, step):
        return pltpu.make_async_remote_copy(
            src_ref=final.at[p], dst_ref=shares_out.at[p, g],
            send_sem=grp_send.at[p, step], recv_sem=grp_recv.at[p, g],
            device_id=((g + step) % groups, f), device_id_type=MESH,
        )

    def grp_wait(p, other):
        pltpu.make_async_remote_copy(
            src_ref=final.at[p], dst_ref=shares_out.at[p, other],
            send_sem=grp_send.at[p, 0], recv_sem=grp_recv.at[p, other],
            device_id=(g, mate), device_id_type=MESH,
        ).wait_recv()

    def keep_copy(p):
        return pltpu.make_async_copy(final.at[p], shares_out.at[p, g], keep_sem.at[p])

    def finish_piece(p):
        mate_copy(p, last).wait_recv()
        own_part[p, last] += from_mate[p, last].astype(F32)

        @pl.when(has_left)
        def _():
            own_part[p, last] += run_wait(p, 1, 0)

        @pl.when(has_right)
        def _():
            own_part[p, last] += run_wait(p, -1, 0)

        final[p] = own_part[p, last].astype(BF16)
        for step in range(1, groups):
            grp_copy(p, step).start()
        keep_copy(p).start()

    load_a.wait()
    wd[f] = jnp.concatenate([a_f32[u].astype(BF16) for u in used], axis=0)
    pl.semaphore_wait(
        barrier, groups + jnp.where(has_left, 1, 0) + jnp.where(has_right, 1, 0)
    )
    gather_own(0)
    load_b.wait()
    for half in range(2):
        maps[1 + half][f] = jnp.concatenate(
            [b_f32[u, :, half * wp:(half + 1) * wp].astype(BF16) for u in used], axis=0
        )
    @pl.when(at_end)
    def _():
        gather_own(1)
        gather_own(2)

    for s in range(shards):
        load_tok(s).start()
    for s in range(shards):
        load_cot(s).start()
    acc[...] = jnp.zeros_like(acc)
    gather_span(0, 0, 2)
    pl.when(jnp.logical_not(at_end))(lambda: gather_own(1))
    gather_span(0, 2, 4 * line)
    pl.when(jnp.logical_not(at_end))(lambda: gather_own(2))
    for s in range(shards):
        load_tok(s).wait()
    accumulate(0)
    low = masked(acc[...])
    low_out[...] = low.astype(BF16)
    left_t[...] = low.T.astype(BF16)
    for s in range(shards):
        load_cot(s).wait()
    partials((0, 1), cot)

    acc[...] = jnp.zeros_like(acc)
    gather_span(1, 0, 4 * line)
    pl.when(at_end)(lambda: accumulate(1))
    gather_span(2, 0, 4 * line)

    @pl.when(jnp.logical_not(at_end))
    def _():
        pass_on((0, 1))
        accumulate(1)

    accumulate(2)
    back = masked(acc[...])
    back_out[...] = back.astype(BF16)
    left_t[...] = back.T.astype(BF16)
    partials((2,), tok)

    store_d = pltpu.make_async_copy(wd, wd_out, store_sem.at[0])
    store_l = pltpu.make_async_copy(wu_low, wu_out.at[0], store_sem.at[1])
    store_h = pltpu.make_async_copy(wu_high, wu_out.at[1], store_sem.at[2])
    store_d.start()
    store_l.start()
    store_h.start()

    finish_piece(0)
    finish_piece(1)
    pl.when(jnp.logical_not(at_end))(lambda: pass_on((2,)))

    names = [
        used_adapters(bm, other * group_blocks, group_blocks, adapters - 1)
        for other in range(groups)
    ]
    owned = [jnp.int32(-1)] * OWN_MAX
    position = jnp.int32(0)
    for a in range(adapters):
        mine = owners[a] == g
        for k in range(OWN_MAX):
            owned[k] = jnp.where(mine & (position == k), a, owned[k])
        position = position + jnp.where(mine, 1, 0)

    def count(i, totals):
        entry = bm[i]
        return tuple(n + jnp.where(entry == o, 1, 0) for n, o in zip(totals, owned))

    totals = lax.fori_loop(0, total_blocks, count, (jnp.int32(0),) * OWN_MAX, unroll=8)
    shape = (OWN_MAX * RANK, groups * ROWS)
    row = lax.broadcasted_iota(jnp.int32, shape, 0)
    col = lax.broadcasted_iota(jnp.int32, shape, 1)
    row_name = jnp.full(shape, -1, jnp.int32)
    col_name = jnp.full(shape, -2, jnp.int32)
    for k in range(OWN_MAX):
        row_name = jnp.where(row // RANK == k, owned[k], row_name)
    for q in range(groups * USED):
        col_name = jnp.where(col // RANK == q, names[q // USED][q % USED], col_name)
    hit = (row % RANK == col % RANK) & (row_name == col_name)
    pick_out[...] = jnp.where(hit, 1.0, 0.0).astype(BF16)
    wide = lax.broadcasted_iota(jnp.int32, scale_out.shape, 0) // RANK
    uses = jnp.zeros(scale_out.shape, jnp.int32)
    for k in range(OWN_MAX):
        uses = jnp.where(wide == k, totals[k], uses)
    scale_out[...] = 1.0 / (BLOCK * jnp.maximum(uses, 1)).astype(F32)

    finish_piece(2)
    for piece in range(PIECES):
        gather_finish(piece)

    for i, step in enumerate(steps):
        @pl.when(here(step))
        def _():
            for p in range(PIECES):
                mate_copy(p, i).wait_send()
                if i != last:
                    run_copy(p, *step).wait_send()

    store_d.wait()
    store_l.wait()
    store_h.wait()
    for p in range(PIECES):
        keep_copy(p).wait()
        for step in range(1, groups):
            grp_copy(p, step).wait_send()
        for step in range(1, groups):
            grp_wait(p, (g + step) % groups)


def outputs(
    low, back, pick, scale, wd, wu, up_shares, down_shares,
    delta, grad_tokens, grad_down, grad_up,
):
    count, _, wp = wd.shape
    for s in range(count):
        for half in range(2):
            start = (s * 2 + half) * wp
            delta[:, start:start + wp] = jnp.dot(
                low[...], wu[half, s], preferred_element_type=F32
            ).astype(delta.dtype)
        grad_tokens[:, s * wp:(s + 1) * wp] = jnp.dot(
            back[...], wd[s], preferred_element_type=F32
        ).astype(grad_tokens.dtype)
    for shares, grad in ((down_shares, grad_down), (up_shares, grad_up)):
        total = jnp.dot(pick[...], shares[0], preferred_element_type=F32)
        grad[...] = (total * scale[:, 0:1]).reshape(grad.shape)


def on_device(groups, shards, tokens, cotangent, adapter_a, adapter_b, block_map, adapter_owner):
    rows, width = tokens.shape
    hidden = cotangent.shape[1]
    wp = adapter_a.shape[2]
    assert adapter_b.shape[2] == 2 * wp
    line = shards // 2
    dma = pltpu.SemaphoreType.DMA
    vmem = pl.BlockSpec(memory_space=pltpu.VMEM)
    smem = pl.BlockSpec(memory_space=pltpu.SMEM)
    anywhere = pl.BlockSpec(memory_space=pl.ANY)
    low, back, pick, scale, wd, wu, shares = pl.pallas_call(
        functools.partial(exchange, groups, shards),
        name="exchange",
        out_shape=(
            jax.ShapeDtypeStruct((rows, ROWS), BF16),
            jax.ShapeDtypeStruct((rows, ROWS), BF16),
            jax.ShapeDtypeStruct((OWN_MAX * RANK, groups * ROWS), BF16),
            jax.ShapeDtypeStruct((OWN_MAX * RANK, 128), F32),
            jax.ShapeDtypeStruct((shards, ROWS, wp), BF16),
            jax.ShapeDtypeStruct((2, shards, ROWS, wp), BF16),
            jax.ShapeDtypeStruct((PIECES, groups, ROWS, wp), BF16),
        ),
        in_specs=[smem, smem] + [anywhere] * 4,
        out_specs=(vmem,) * 4 + (anywhere,) * 3,
        scratch_shapes=[
            pltpu.VMEM(adapter_a.shape, F32),
            pltpu.VMEM(adapter_b.shape, F32),
            pltpu.VMEM((shards, ROWS, wp), BF16),
            pltpu.VMEM((shards, ROWS, wp), BF16),
            pltpu.VMEM((shards, ROWS, wp), BF16),
            pltpu.VMEM((shards, rows, wp), BF16),
            pltpu.VMEM((shards, rows, 2 * wp), BF16),
            pltpu.VMEM((rows, ROWS), F32),
            pltpu.VMEM((ROWS, rows), BF16),
            pltpu.VMEM((PIECES, 2 * line - 1, ROWS, wp), BF16),
            pltpu.VMEM((PIECES, 2 * line - 1, ROWS, wp), BF16),
            pltpu.VMEM((PIECES, 2 * line - 1, ROWS, wp), F32),
            pltpu.VMEM((PIECES, 2, line, ROWS, wp), BF16),
            pltpu.VMEM((PIECES, 2 * line - 1, ROWS, wp), BF16),
            pltpu.VMEM((PIECES, ROWS, wp), BF16),
            dma((2,)),
            dma((shards,)),
            dma((shards,)),
            dma((3,)),
            dma((3, PIECES, line)),
            dma((PIECES, shards)),
            dma((PIECES, 2 * line - 1)),
            dma((PIECES, 2 * line - 1)),
            dma((PIECES, 2 * line - 1)),
            dma((PIECES, 2, line)),
            dma((PIECES, groups)),
            dma((PIECES, groups)),
            dma((PIECES,)),
        ],
        compiler_params=pltpu.CompilerParams(
            collective_id=0, has_side_effects=True, vmem_limit_bytes=56 * 1024 * 1024
        ),
    )(block_map, adapter_owner, adapter_a, adapter_b, tokens, cotangent)
    shares = shares.reshape(PIECES, groups * ROWS, wp)
    steps = min(4, wp // 128)
    half = steps // 2
    whole = lambda shape: pl.BlockSpec(shape, lambda i: (0,) * len(shape))
    return pl.pallas_call(
        outputs,
        name="outputs",
        grid=(steps,),
        out_shape=(
            jax.ShapeDtypeStruct((rows, hidden), BF16),
            jax.ShapeDtypeStruct((rows, width), BF16),
            jax.ShapeDtypeStruct((OWN_MAX, RANK, wp), F32),
            jax.ShapeDtypeStruct((OWN_MAX, RANK, 2 * wp), F32),
        ),
        in_specs=[
            whole(low.shape), whole(back.shape), whole(pick.shape), whole(scale.shape),
            pl.BlockSpec((shards // steps, ROWS, wp), lambda i: (i, 0, 0)),
            pl.BlockSpec((2, shards // steps, ROWS, wp), lambda i: (0, i, 0, 0)),
            pl.BlockSpec((1, groups * ROWS, wp // half), lambda i: (i // half, 0, i % half)),
            pl.BlockSpec((1, groups * ROWS, wp // steps), lambda i: (2, 0, i)),
        ],
        out_specs=(
            pl.BlockSpec((rows, hidden // steps), lambda i: (0, i)),
            pl.BlockSpec((rows, width // steps), lambda i: (0, i)),
            pl.BlockSpec((OWN_MAX, RANK, wp // steps), lambda i: (0, 0, i)),
            pl.BlockSpec((OWN_MAX, RANK, 2 * wp // steps), lambda i: (0, 0, i)),
        ),
    )(low, back, pick, scale, wd, wu, shares, shares)


def solution(mesh):
    placed = (
        P(("grp", "fsdp"), None),
        P(("grp", "fsdp"), None),
        P(None, None, "fsdp"),
        P(None, None, "fsdp"),
        P(),
        P(),
    )
    return jax.shard_map(
        functools.partial(on_device, mesh.shape["grp"], mesh.shape["fsdp"]),
        mesh=mesh,
        in_specs=placed,
        out_specs=(
            P(("grp", "fsdp"), None),
            P(("grp", "fsdp"), None),
            P("grp", None, "fsdp"),
            P("grp", None, "fsdp"),
        ),
        check_vma=False,
    )
```
